32 devices in a mesh: groups: 2 (over y), bond: 8 (over z, x), section: 2 (over core).
Axes of the slice: x: 2, y: 2, z: 4, core: 2. Of those that a mesh axis runs over, the one named last changes fastest.
Arguments:
- environment: float32 [2, 4096, 512], P(None, 'bond', 'groups'), parts along dimension 2, may hold values from -30 to 30
- outcomes: int32 [2, 2, 512], P('section', None, 'groups'), parts along dimension 2, may hold values from 0 to 3
- tensors: bfloat16 [2, 4, 4096, 4096], P('section', None, 'bond'), may hold values from -0.09375 to 0.09375
Outputs:
- section_envs: float32 [2, 2, 4096, 512], P('section', None, 'bond', 'groups'), parts along dimension 3
- log_scale: float32 [2, 2, 512], P('section', None, 'groups'), parts along dimension 2
The draws below stay inside these ranges and needn't reach their ends.
There are 2 independent parts, one for each index of `groups`. The reference program is written for one: setup_inputs(seed, part) draws one part's arguments, and reference() takes and returns one part's arrays. A program takes and returns all parts, laid end to end along the dimension named above; an argument that names none is the same for every part. Nothing has to cross between parts.
All inputs are finite; a program needn't handle non-finite values.
Results may differ from the reference program's by a relative error of at most 0.0035.
Values may be sent and summed in bfloat16 or wider, within the bound.
A program may use at most 64 MiB of HBM per device.

```python
import math
import jax
import jax.numpy as jnp
from jax import lax

CHI = 4096
OUT = 4
ROWS = 256
MB = 2
MODES = 2


def draw_environment(key, part):
    first_key, second_key = jax.random.split(jax.random.fold_in(key, 11))
    base = jnp.clip(jax.random.normal(first_key, (MB, CHI, ROWS), jnp.float32), -6.0, 6.0)
    factor = jnp.exp(jax.random.uniform(second_key, (MB, 1, ROWS), jnp.float32, math.log(0.2), math.log(5.0)))
    return (base * factor).astype(jnp.float32)


def place_ends(drawn, own_key, low, high):
    longest = drawn.shape.index(max(drawn.shape))
    spots = []
    for shift in (0, 1):
        where = [jax.random.randint(jax.random.fold_in(own_key, axis), (), 0, length) for axis, length in enumerate(drawn.shape)]
        where[longest] = (where[longest] + shift) % drawn.shape[longest]
        spots.append(tuple(where))
    return drawn.at[spots[0]].set(low).at[spots[1]].set(high)


def block_scale(own_key, shape, cuts, low, top_value):
    gain = 1.0
    for dim, parts in cuts:
        draws = jax.random.uniform(jax.random.fold_in(jax.random.fold_in(own_key, 6), dim), (parts,), jnp.float32, low / len(cuts), top_value / len(cuts))
        gain = gain * jnp.repeat(jnp.exp(draws), shape[dim] // parts).reshape((-1,) + (1,) * (len(shape) - 1 - dim))
    return gain


def bell_draw(own_key, shape, width, bound, pieces=(), kind=jnp.bfloat16):
    entries = jax.random.normal(own_key, shape, jnp.float32) * width
    if len(pieces) > 0:
        entries = block_scale(own_key, shape, pieces, -0.22, 0.18) * entries
    return jnp.clip(entries, min=-bound, max=bound).astype(kind)


def setup_inputs(seed: int = 0, part: int = 0) -> dict:
    splits = jax.random.split(jax.random.key(seed), 4)
    own_keys = jax.random.split(jax.random.fold_in(splits[3], part), 4)
    environment = draw_environment(jax.random.fold_in(jax.random.fold_in(splits[3], part), 71), part)
    outcomes = place_ends(jax.random.randint(own_keys[1], (MODES, MB, ROWS), 0, OUT), jax.random.fold_in(own_keys[1], 1), 0, OUT - 1).astype(jnp.int32)
    tensors = bell_draw(splits[2], (MODES, OUT, CHI, CHI), CHI ** -0.5, 0.09375, ((0, 2), (2, 8)))
    return {"environment": environment, "outcomes": outcomes, "tensors": tensors}


def reference(environment, outcomes, tensors):
    current = environment
    accumulated = jnp.zeros((MB, ROWS), jnp.float32)
    env_list = []
    log_list = []
    levels = jnp.arange(OUT, dtype=jnp.int32)
    for mode_index in range(MODES):
        resident = tensors[mode_index].astype(jnp.float32)
        rounded = current.astype(jnp.bfloat16).astype(jnp.float32)
        every = jnp.einsum('oki,bir->bokr', resident, rounded, precision=lax.Precision.HIGHEST)
        picked = (outcomes[mode_index][:, None, :] == levels[None, :, None]).astype(jnp.float32)
        product = lax.optimization_barrier(jnp.sum(every * picked[:, :, None, :], axis=1))
        scale = jnp.sqrt(lax.optimization_barrier(jnp.mean(product * product, axis=1)) + 1e-06)
        current = product / scale[:, None, :]
        accumulated = accumulated + jnp.log(scale)
        env_list.append(current)
        log_list.append(accumulated)
    return (jnp.stack(env_list), jnp.stack(log_list))
```

```python
import functools
import math
import jax
import jax.numpy as jnp
from jax import lax
from jax.experimental import pallas as pl
from jax.experimental.pallas import tpu as pltpu
from jax.sharding import PartitionSpec as P

MESH = pl.DeviceIdType.MESH
LIFT = 1024.0
EPS = 1e-06
UNROLL = 8


def steps(start, stop, body):
    if stop - start <= UNROLL:
        for k in range(start, stop):
            body(k)
    else:
        def wrapped(k, carry):
            body(k)
            return carry
        lax.fori_loop(start, stop, wrapped, 0)


def outward(k, pos, size):
    near = jnp.minimum(pos, size - 1 - pos)
    half = (k + 1) // 2
    both = pos + jnp.where(k % 2 == 1, half, -half)
    single = jnp.where(pos <= size - 1 - pos, k, size - 1 - k)
    return jnp.where(k <= 2 * near, both, single)


def kernel(dims, codes_ref, env_ref, w_ref, prod_ref, factor_ref, log_ref,
           gathered, wbuf, envbuf, acc, passed, sums,
           env_sem, w_sem, out_sem, recv, own_x, own_z, pass_x, pass_z, relay, relay_z,
           sum_recv, sum_send):
    n, line, side, pieces, per_chunk, batches, outs, rows, cols = dims
    full_bond = n * rows
    me = lax.axis_index("bond")
    sec = lax.axis_index("section")
    my_z, my_x = me // side, me % side
    part = rows // pieces
    chunk_rows = per_chunk * rows
    chunks_row = side // per_chunk
    first = sec == 0

    def z_of(k):
        return outward(k, my_z, line)

    def x_of(k):
        return outward(k, my_x, side)

    def beside(k):
        return my_z + 2 * k - 1

    def on_line(z):
        return jnp.logical_and(z >= 0, z < line)

    def chunk_start(kz, kx):
        z = z_of(kz)
        return z * side + (x_of(kx) if per_chunk == 1 else 0)

    def piece(b, src, p):
        return gathered.at[b, src, pl.ds(p * part, part)]

    def send(src_ref, b, src, p, sem, bond, section):
        return pltpu.make_async_remote_copy(
            src_ref=src_ref, dst_ref=piece(b, src, p), send_sem=sem, recv_sem=recv.at[b, src, p],
            device_id={"bond": bond, "section": section}, device_id_type=MESH)

    def own_copy(b, p, k, along):
        if along == "x":
            return send(piece(b, me, p), b, me, p, own_x.at[b, k, p], my_z * side + x_of(k), 0)
        return send(piece(b, me, p), b, me, p, own_z.at[b, k, p], beside(k) * side + my_x, 0)

    def pass_copy(b, p, k, along):
        src = passed.at[b, pl.ds(p * part, part)]
        if along == "x":
            return send(src, b, me, p, pass_x.at[b, k, p], my_z * side + x_of(k), 1)
        return send(src, b, me, p, pass_z.at[b, k, p], beside(k) * side + my_x, 1)

    def relay_copy(b, p, kz, kx):
        src = z_of(kz) * side + my_x
        return send(piece(b, src, p), b, src, p, relay.at[b, kz, kx, p], my_z * side + x_of(kx), sec)

    def beyond(kz):
        return my_z + jnp.where(z_of(kz) < my_z, 1, -1)

    def relay_z_copy(b, p, kz):
        src = z_of(kz) * side + my_x
        return send(piece(b, src, p), b, src, p, relay_z.at[b, kz, p], beyond(kz) * side + my_x, sec)

    def relay_x(b, p, kz, act):
        steps(1, side, lambda kx: act(relay_copy(b, p, kz, kx)))

    def relay_line(b, p, kz, act):
        @pl.when(on_line(beyond(kz)))
        def _():
            act(relay_z_copy(b, p, kz))

    def both_sides(b, p, copy, act):
        for k in range(2):
            @pl.when(on_line(beside(k)))
            def _():
                act(copy(b, p, k, "z"))

    def start(copy):
        copy.start()

    def sent(copy):
        copy.wait_send()

    def await_piece(b, src, p):
        send(piece(b, src, p), b, src, p, own_x.at[b, 0, p], me, 1 - sec).wait_recv()

    def w_copy(kz, kx):
        at = pl.multiple_of(chunk_start(kz, kx) * rows, 128)
        return pltpu.make_async_copy(
            w_ref.at[:, :, pl.ds(at, chunk_rows)], wbuf.at[kz * chunks_row + kx], w_sem.at[kz * chunks_row + kx])

    def env_copy(b):
        return pltpu.make_async_copy(env_ref.at[b], envbuf.at[b], env_sem.at[b])

    def out_copy(b):
        return pltpu.make_async_copy(acc.at[b], prod_ref.at[b], out_sem.at[b])

    @pl.when(first)
    def _():
        for b in range(batches):
            env_copy(b).start()

    def start_w():
        def row_w(kz):
            for kx in range(chunks_row):
                w_copy(kz, kx).start()
        steps(0, line, row_w)

    pl.when(jnp.logical_not(first))(start_w)

    barrier = pltpu.get_barrier_semaphore()

    def neighbours(act):
        act(None, {"bond": me, "section": 1 - sec})
        for k in range(1, side):
            for section in range(2):
                act(None, {"bond": my_z * side + x_of(k), "section": section})
        for k in range(2):
            for section in range(2):
                act(on_line(beside(k)), {"bond": beside(k) * side + my_x, "section": section})

    def greet(there, who):
        def signal():
            pl.semaphore_signal(barrier, inc=1, device_id=who, device_id_type=MESH)
        signal() if there is None else pl.when(there)(signal)

    neighbours(greet)

    @pl.when(first)
    def _():
        for b in range(batches):
            env_copy(b).wait()
            gathered[b, me] = envbuf[b].astype(jnp.bfloat16)
    ends = jnp.where(my_z == 0, 1, 0) + jnp.where(my_z == line - 1, 1, 0)
    pl.semaphore_wait(barrier, 1 + 2 * (side - 1) + 2 * (2 - ends))

    def own_sends(b):
        for p in range(pieces):
            both_sides(b, p, own_copy, start)
            steps(1, side, lambda k: own_copy(b, p, k, "x").start())

    @pl.when(first)
    def _():
        own_sends(0)
        start_w()

    def forward(b, kz):
        src = z_of(kz) * side + my_x
        for p in range(pieces):
            await_piece(b, src, p)
            relay_line(b, p, kz, start)
            relay_x(b, p, kz, start)

    def await_shard(b, kz, kx):
        for p in range(pieces):
            await_piece(b, z_of(kz) * side + x_of(kx), p)

    def multiply(b, kz, kx, fresh):
        if b == 0:
            w_copy(kz, kx).wait()
        base = chunk_start(kz, kx)
        if per_chunk == 1:
            value = gathered[b, base]
        else:
            value = gathered[b, pl.ds(base, per_chunk)].reshape(chunk_rows, cols)
        at = kz * chunks_row + kx
        total = None
        for o in range(outs):
            chosen = jnp.where(codes_ref[pl.ds(b, 1), :] == o, 1.0, 0.0).astype(jnp.bfloat16)
            term = jnp.dot(wbuf[at, o], value * chosen, preferred_element_type=jnp.float32)
            total = term if total is None else total + term
        if fresh:
            acc[b] = total
        else:
            acc[b] += total

    def sum_copy(kind, b, o, section):
        peer = lax.rem(me + o, n)
        return pltpu.make_async_remote_copy(
            src_ref=sums.at[kind, b, me], dst_ref=sums.at[kind, b, me],
            send_sem=sum_send.at[section, b, o], recv_sem=sum_recv.at[kind, b, me],
            device_id={"bond": peer, "section": section}, device_id_type=MESH)

    def await_sum(kind, b, src):
        pltpu.make_async_remote_copy(
            src_ref=sums.at[kind, b, src], dst_ref=sums.at[kind, b, src],
            send_sem=sum_send.at[0, b, 0], recv_sem=sum_recv.at[kind, b, src],
            device_id={"bond": me, "section": 1 - sec}, device_id_type=MESH).wait_recv()

    def row(b, kz):
        fresh = isinstance(kz, int) and kz == 0
        if per_chunk == 1:
            for kx in range(side):
                if kx > 0 and not fresh:
                    await_shard(b, kz, kx)
                multiply(b, kz, kx, fresh and kx == 0)
        else:
            if not fresh:
                steps(1, side, lambda kx: await_shard(b, kz, kx))
            multiply(b, kz, 0, fresh)

    def await_own(b):
        @pl.when(jnp.logical_not(first))
        def _():
            for p in range(pieces):
                await_piece(b, me, p)

    def own_column(b, kz):
        multiply(b, kz, 0, isinstance(kz, int) and kz == 0)

    def other_columns(b, kz):
        for kx in range(1, side):
            await_shard(b, kz, kx)
            multiply(b, kz, kx, False)

    def next_own(b):
        if b + 1 < batches:
            @pl.when(first)
            def _():
                own_sends(b + 1)

    def next_forward(b):
        if b + 1 < batches and line > 1:
            forward(b + 1, 1)

    for b in range(batches):
        if line > 1 and b == 0:
            forward(b, 1)
        await_own(b)
        if per_chunk == 1 and line <= UNROLL:
            own_column(b, 0)
            for kz in range(2, line):
                forward(b, kz)
                if kz == line - 1:
                    next_own(b)
                other_columns(b, kz - 2)
                own_column(b, kz - 1)
            if line <= 2:
                next_own(b)
            for kz in range(max(line - 2, 0), line):
                if kz > 0 and kz == line - 1:
                    own_column(b, kz)
                    next_forward(b)
                other_columns(b, kz)
        else:
            steps(1, side, lambda kx: await_shard(b, 0, kx))
            steps(2, line, lambda kz: forward(b, kz))
            next_own(b)
            row(b, 0)
            steps(1, line - 1, lambda kz: row(b, kz))
            if line > 1:
                next_forward(b)
                row(b, line - 1)

        product = acc[b]

        @pl.when(first)
        def _():
            passed[b] = (product * LIFT).astype(jnp.bfloat16)
            for p in range(pieces):
                pass_copy(b, p, 0, "x").start()
                steps(1, side, lambda k: pass_copy(b, p, k, "x").start())
                both_sides(b, p, pass_copy, start)

        squares = jnp.sum(product * product, axis=0, keepdims=True)

        @pl.when(first)
        def _():
            sums[0, b, me] = squares
            steps(1, n, lambda o: sum_copy(0, b, o, 0).start())
            steps(0, n, lambda o: sum_copy(0, b, o, 1).start())

        @pl.when(jnp.logical_not(first))
        def _():
            sums[1, b, me] = squares
            steps(1, n, lambda o: sum_copy(1, b, o, 1).start())
        out_copy(b).start()

    def total_of(kind, b, own):
        steps(0 if not own else 1, n, lambda o: await_sum(kind, b, lax.rem(me + o, n)))
        return jnp.sum(sums[kind, b], axis=0)

    @pl.when(first)
    def _():
        for b in range(batches):
            scale = jnp.sqrt(total_of(0, b, True) / full_bond + EPS)
            factor_ref[pl.ds(b, 1), :] = 1.0 / scale
            log_ref[pl.ds(b, 1), :] = jnp.log(scale)

    @pl.when(jnp.logical_not(first))
    def _():
        for b in range(batches):
            before = jnp.sqrt(total_of(0, b, False) / full_bond + EPS)
            inner = 1.0 / (before * LIFT)
            scale = jnp.sqrt(total_of(1, b, True) * (inner * inner) / full_bond + EPS)
            factor_ref[pl.ds(b, 1), :] = inner / scale
            log_ref[pl.ds(b, 1), :] = jnp.log(before) + jnp.log(scale)

    for b in range(batches):
        out_copy(b).wait()
        for p in range(pieces):
            def drain(kz):
                relay_x(b, p, kz, sent)
                relay_line(b, p, kz, sent)
            steps(1, line, drain)

        @pl.when(first)
        def _():
            for p in range(pieces):
                steps(1, side, lambda k: own_copy(b, p, k, "x").wait_send())
                both_sides(b, p, own_copy, sent)
                steps(0, side, lambda k: pass_copy(b, p, k, "x").wait_send())
                both_sides(b, p, pass_copy, sent)
            steps(1, n, lambda o: sum_copy(0, b, o, 0).wait_send())
            steps(0, n, lambda o: sum_copy(0, b, o, 1).wait_send())

        @pl.when(jnp.logical_not(first))
        def _():
            steps(1, n, lambda o: sum_copy(1, b, o, 1).wait_send())


def pair_kernel(dims, codes_ref, env_ref, w_ref, prod_ref, factor_ref, log_ref,
                gathered, wbuf, envbuf, acc, passed, sums,
                env_sem, w_sem, out_sem, recv, own_sem, pass_sem, relay_sem, onward_sem, swap_sem,
                sum_recv, sum_send):
    n, line, batches, outs, rows, cols = dims
    side, pieces = 2, 4
    part, span = rows // pieces, rows // 2
    me = lax.axis_index("bond")
    sec = lax.axis_index("section")
    my_z, my_x = me // side, me % side
    first = sec == 0

    low = my_z < line // 2
    inner = jnp.logical_and(my_z > 0, my_z < line - 1)
    rows_near = (my_z, my_z + 1 - 2 * (my_z % 2), jnp.where(low, 2, 1), jnp.where(low, 3, 0))

    def row_of(k):
        return rows_near[k]

    def column(k):
        return row_of(k) * side + my_x

    def across(k):
        return row_of(k) * side + 1 - my_x

    blocks = [(me, half) for half in range(2)]
    blocks += [(column(k), half) for half in range(2) for k in range(1, line)]
    blocks += [(across(k), half) for half in range(2) for k in range(line)]

    def column_slot(k, half):
        return 2 + half * (line - 1) + k - 1

    def across_slot(k, half):
        return 2 * line + half * line + k

    def piece(b, src, p):
        return gathered.at[b, src, pl.ds(p * part, part)]

    def send(src_ref, b, src, p, sem, bond, section):
        return pltpu.make_async_remote_copy(
            src_ref=src_ref, dst_ref=piece(b, src, p), send_sem=sem, recv_sem=recv.at[b, src, p],
            device_id={"bond": bond, "section": section}, device_id_type=MESH)

    def own_copy(b, p, k):
        return send(piece(b, me, p), b, me, p, own_sem.at[b, k, p], across(0) if k == 0 else column(k), 0)

    def pass_copy(b, p, k):
        src = passed.at[b, pl.ds(p * part, part)]
        bond = me if k == line else across(0) if k == 0 else column(k)
        return send(src, b, me, p, pass_sem.at[b, k, p], bond, 1)

    def relay_copy(b, k, p):
        return send(piece(b, column(k), p), b, column(k), p, relay_sem.at[b, k, p], across(0), sec)

    def onward_copy(b, p):
        return send(piece(b, column(3), p), b, column(3), p, onward_sem.at[b, p], column(1), sec)

    def swap_copy(b, p):
        return send(piece(b, across(0), p), b, across(0), p, swap_sem.at[b, p], column(1), sec)

    def direct(copy, b, p, k, act):
        if k == 3:
            pl.when(inner)(lambda: act(copy(b, p, k)))
        else:
            act(copy(b, p, k))

    def start(copy):
        copy.start()

    def sent(copy):
        copy.wait_send()

    def await_piece(b, src, p):
        send(piece(b, src, p), b, src, p, own_sem.at[b, 0, 0], me, 1 - sec).wait_recv()

    def w_copies(slot):
        src, half = blocks[slot]
        at = pl.multiple_of(src * rows + half * span, 128)
        return [pltpu.make_async_copy(
            w_ref.at[o, :, pl.ds(at, span)], wbuf.at[slot, :, pl.ds(o * span, span)],
            w_sem.at[slot, o]) for o in range(outs)]

    def start_w():
        for slot in range(2 * n):
            for copy in w_copies(slot):
                copy.start()

    def env_copy(b):
        return pltpu.make_async_copy(env_ref.at[b], envbuf.at[b], env_sem.at[b])

    def out_copy(b):
        return pltpu.make_async_copy(acc.at[b], prod_ref.at[b], out_sem.at[b])

    @pl.when(first)
    def _():
        for b in range(batches):
            env_copy(b).start()

    pl.when(jnp.logical_not(first))(start_w)

    barrier = pltpu.get_barrier_semaphore()

    def greet(who):
        pl.semaphore_signal(barrier, inc=1, device_id=who, device_id_type=MESH)

    greet({"bond": me, "section": 1 - sec})
    for section in range(2):
        greet({"bond": across(0), "section": section})
        for k in range(1, line):
            greet({"bond": column(k), "section": section})

    @pl.when(first)
    def _():
        env_copy(0).wait()
        gathered[0, me] = envbuf[0].astype(jnp.bfloat16)

    pl.semaphore_wait(barrier, 2 * line + 1)

    def column_sends(b):
        for p in range(pieces):
            for k in range(1, line):
                direct(own_copy, b, p, k, start)
            if b == 0:
                own_copy(b, p, 0).start()

    @pl.when(first)
    def _():
        column_sends(0)
        start_w()
        for b in range(1, batches):
            env_copy(b).wait()
            gathered[b, me] = envbuf[b].astype(jnp.bfloat16)
            column_sends(b)

    def across_sends(b):
        if b < batches:
            @pl.when(first)
            def _():
                for p in range(pieces):
                    own_copy(b, p, 0).start()

    def forward(b, k, half):
        for p in range(2 * half, 2 * half + 2):
            await_piece(b, column(k), p)
            if k == 3:
                pl.when(inner)(lambda: onward_copy(b, p).start())
            if k > 1 or half == 0:
                relay_copy(b, k, p).start()

    def arrived(b, k, half):
        for p in range(2 * half, 2 * half + 2):
            await_piece(b, across(k), p)
            if k == 0 and half == 1:
                swap_copy(b, p).start()
        multiply(b, across_slot(k, half))

    def multiply(b, slot):
        src, half = blocks[slot]
        if b == 0:
            for copy in w_copies(slot):
                copy.wait()
        value = gathered[b, src, pl.ds(half * span, span)]
        chosen = [jnp.where(codes_ref[pl.ds(b, 1), :] == o, 1.0, 0.0).astype(jnp.bfloat16) for o in range(outs)]
        stacked = jnp.concatenate([value * c for c in chosen], axis=0)
        term = jnp.dot(wbuf[slot], stacked, preferred_element_type=jnp.float32)
        if slot == 0:
            acc[b] = term
        else:
            acc[b] += term

    def sum_copy(kind, b, o, section):
        peer = lax.rem(me + o, n)
        return pltpu.make_async_remote_copy(
            src_ref=sums.at[kind, b, me], dst_ref=sums.at[kind, b, me],
            send_sem=sum_send.at[section, b, o], recv_sem=sum_recv.at[kind, b, me],
            device_id={"bond": peer, "section": section}, device_id_type=MESH)

    def await_sum(kind, b, src):
        pltpu.make_async_remote_copy(
            src_ref=sums.at[kind, b, src], dst_ref=sums.at[kind, b, src],
            send_sem=sum_send.at[0, b, 0], recv_sem=sum_recv.at[kind, b, src],
            device_id={"bond": me, "section": 1 - sec}, device_id_type=MESH).wait_recv()

    for b in range(batches):
        forward(b, 1, 0)
        @pl.when(jnp.logical_not(first))
        def _():
            for p in range(pieces):
                await_piece(b, me, p)
        multiply(b, 0)
        multiply(b, 1)
        forward(b, 2, 0)
        multiply(b, column_slot(1, 0))
        multiply(b, column_slot(2, 0))
        arrived(b, 0, 0)
        arrived(b, 0, 1)
        forward(b, 3, 0)
        multiply(b, column_slot(3, 0))
        for k in range(1, line):
            forward(b, k, 1)
            multiply(b, column_slot(k, 1))
        across_sends(b + 1)
        for half in range(2):
            for k in range(1, line):
                arrived(b, k, half)

        @pl.when(first)
        def _():
            for p in range(pieces):
                at = pl.ds(p * part, part)
                passed[b, at] = (acc[b, at] * LIFT).astype(jnp.bfloat16)
                pass_copy(b, p, line).start()
                for k in range(line):
                    direct(pass_copy, b, p, k, start)

        product = acc[b]
        squares = jnp.sum(product * product, axis=0, keepdims=True)

        @pl.when(first)
        def _():
            sums[0, b, me] = squares
            steps(1, n, lambda o: sum_copy(0, b, o, 0).start())
            steps(0, n, lambda o: sum_copy(0, b, o, 1).start())

        @pl.when(jnp.logical_not(first))
        def _():
            sums[1, b, me] = squares
            steps(1, n, lambda o: sum_copy(1, b, o, 1).start())
        out_copy(b).start()

    def total_of(kind, b, own):
        steps(0 if not own else 1, n, lambda o: await_sum(kind, b, lax.rem(me + o, n)))
        return jnp.sum(sums[kind, b], axis=0)

    @pl.when(first)
    def _():
        for b in range(batches):
            scale = jnp.sqrt(total_of(0, b, True) / (n * rows) + EPS)
            factor_ref[pl.ds(b, 1), :] = 1.0 / scale
            log_ref[pl.ds(b, 1), :] = jnp.log(scale)

    @pl.when(jnp.logical_not(first))
    def _():
        for b in range(batches):
            before = jnp.sqrt(total_of(0, b, False) / (n * rows) + EPS)
            inner = 1.0 / (before * LIFT)
            scale = jnp.sqrt(total_of(1, b, True) * (inner * inner) / (n * rows) + EPS)
            factor_ref[pl.ds(b, 1), :] = inner / scale
            log_ref[pl.ds(b, 1), :] = jnp.log(before) + jnp.log(scale)

    for b in range(batches):
        out_copy(b).wait()
        for p in range(pieces):
            for k in range(1, line):
                if k > 1 or p < 2:
                    relay_copy(b, k, p).wait_send()
            pl.when(inner)(lambda: onward_copy(b, p).wait_send())
            if p >= 2:
                swap_copy(b, p).wait_send()

        @pl.when(first)
        def _():
            for p in range(pieces):
                for k in range(line):
                    direct(own_copy, b, p, k, sent)
                for k in range(line + 1):
                    direct(pass_copy, b, p, k, sent)
            steps(1, n, lambda o: sum_copy(0, b, o, 0).wait_send())
            steps(0, n, lambda o: sum_copy(0, b, o, 1).wait_send())

        @pl.when(jnp.logical_not(first))
        def _():
            steps(1, n, lambda o: sum_copy(1, b, o, 1).wait_send())


def pair_call(n, batches, outs, rows, cols):
    line = n // 2
    blocks = 2 * n
    dma = pltpu.SemaphoreType.DMA
    vmem = pl.BlockSpec(memory_space=pltpu.VMEM)
    hbm = pl.BlockSpec(memory_space=pltpu.HBM)
    return pl.pallas_call(
        functools.partial(pair_kernel, (n, line, batches, outs, rows, cols)),
        out_shape=(
            jax.ShapeDtypeStruct((batches, rows, cols), jnp.float32),
            jax.ShapeDtypeStruct((batches, cols), jnp.float32),
            jax.ShapeDtypeStruct((batches, cols), jnp.float32),
        ),
        in_specs=[vmem, hbm, hbm],
        out_specs=(hbm, vmem, vmem),
        scratch_shapes=[
            pltpu.VMEM((batches, n, rows, cols), jnp.bfloat16),
            pltpu.VMEM((blocks, rows, outs * rows // 2), jnp.bfloat16),
            pltpu.VMEM((batches, rows, cols), jnp.float32),
            pltpu.VMEM((batches, rows, cols), jnp.float32),
            pltpu.VMEM((batches, rows, cols), jnp.bfloat16),
            pltpu.VMEM((2, batches, n, 1, cols), jnp.float32),
            dma((batches,)),
            dma((blocks, outs)),
            dma((batches,)),
            dma((batches, n, 4)),
            dma((batches, line, 4)),
            dma((batches, line + 1, 4)),
            dma((batches, line, 4)),
            dma((batches, 4)),
            dma((batches, 4)),
            dma((2, batches, n)),
            dma((2, batches, n)),
        ],
        compiler_params=pltpu.CompilerParams(
            collective_id=0, has_side_effects=True, vmem_limit_bytes=56 * 2**20),
    )


def side_of(n):
    side = math.isqrt(n // 2) if n > 1 else 1
    return side if side > 0 and n % side == 0 else 1


def shards(environment, outcomes, tensors):
    n = lax.axis_size("bond")
    batches, rows, cols = environment.shape
    outs = tensors.shape[1]
    side = side_of(n)
    line = n // side
    pieces = 2 if rows % 32 == 0 and rows >= 128 else 1
    per_chunk = 1 if rows % 128 == 0 else side
    n_chunks = n // per_chunk
    if side == 2 and line == 4 and rows % 256 == 0:
        prod, factor, logs = pair_call(n, batches, outs, rows, cols)(outcomes[0], environment, tensors[0])
        return (prod * factor[:, None, :])[None], logs[None]
    dims = (n, line, side, pieces, per_chunk, batches, outs, rows, cols)
    dma = pltpu.SemaphoreType.DMA
    vmem = pl.BlockSpec(memory_space=pltpu.VMEM)
    hbm = pl.BlockSpec(memory_space=pltpu.HBM)
    prod, factor, logs = pl.pallas_call(
        functools.partial(kernel, dims),
        out_shape=(
            jax.ShapeDtypeStruct((batches, rows, cols), jnp.float32),
            jax.ShapeDtypeStruct((batches, cols), jnp.float32),
            jax.ShapeDtypeStruct((batches, cols), jnp.float32),
        ),
        in_specs=[vmem, hbm, hbm],
        out_specs=(hbm, vmem, vmem),
        scratch_shapes=[
            pltpu.VMEM((batches, n, rows, cols), jnp.bfloat16),
            pltpu.VMEM((n_chunks, outs, rows, per_chunk * rows), jnp.bfloat16),
            pltpu.VMEM((batches, rows, cols), jnp.float32),
            pltpu.VMEM((batches, rows, cols), jnp.float32),
            pltpu.VMEM((batches, rows, cols), jnp.bfloat16),
            pltpu.VMEM((2, batches, n, 1, cols), jnp.float32),
            dma((batches,)),
            dma((n_chunks,)),
            dma((batches,)),
            dma((batches, n, pieces)),
            dma((batches, side, pieces)),
            dma((batches, 2, pieces)),
            dma((batches, side, pieces)),
            dma((batches, 2, pieces)),
            dma((batches, line, side, pieces)),
            dma((batches, line, pieces)),
            dma((2, batches, n)),
            dma((2, batches, n)),
        ],
        compiler_params=pltpu.CompilerParams(
            collective_id=0, has_side_effects=True, vmem_limit_bytes=56 * 2**20),
    )(outcomes[0], environment, tensors[0])
    return (prod * factor[:, None, :])[None], logs[None]


def solution(mesh):
    return jax.shard_map(
        shards,
        mesh=mesh,
        in_specs=(
            P(None, "bond", "groups"),
            P("section", None, "groups"),
            P("section", None, "bond", None),
        ),
        out_specs=(P("section", None, "bond", "groups"), P("section", None, "groups")),
        check_vma=False,
    )
```
